32 devices in a mesh: dp: 4 (over y, x), seq: 8 (over z, core).
Axes of the slice: x: 2, y: 2, z: 4, core: 2. Of those that a mesh axis runs over, the one named last changes fastest.
Arguments:
- hidden_in: bfloat16 [8, 2048, 768], P('dp', 'seq'), may hold values from -6 to 6
- segment_ids: int32 [8, 2048], P('dp', 'seq'), may hold values from 0 to 2, never falling along the last dimension, each value on 1 to 1024 neighbouring positions
- cotangent: bfloat16 [8, 2048, 768], P('dp', 'seq'), may hold values from -6 to 6
- norm_gain: float32 [768], replicated, may hold values from 0.5 to 1.5
- in_proj: bfloat16 [768, 3352], replicated, may hold values from -0.21875 to 0.21875
- conv_weight: float32 [4, 1792], replicated, may hold values from -3 to 3
- conv_bias: float32 [1792], replicated, may hold values from -3 to 3
- dt_bias: float32 [24], replicated, may hold values from -4 to 0
- a_log: float32 [24], replicated, may hold values from -8 to 1
- d_skip: float32 [24], replicated, may hold values from 0.5 to 1.5
- mix_gain: float32 [1536], replicated, may hold values from 0.5 to 1.5
- out_proj: bfloat16 [1536, 768], replicated, may hold values from -0.15625 to 0.15625
Outputs:
- hidden_out: bfloat16 [8, 2048, 768], P('dp', 'seq')
- grad_hidden: bfloat16 [8, 2048, 768], P('dp', 'seq')
- grad_norm_gain: float32 [768], replicated
- grad_in_proj: float32 [768, 3352], replicated
- grad_conv_weight: float32 [4, 1792], replicated
- grad_conv_bias: float32 [1792], replicated
- grad_dt_bias: float32 [24], replicated
- grad_a_log: float32 [24], replicated
- grad_d_skip: float32 [24], replicated
- grad_mix_gain: float32 [1536], replicated
- grad_out_proj: float32 [1536, 768], replicated
The draws below stay inside these ranges and needn't reach their ends.
Inputs may be any that keep to these rules, and one draw needn't show every extreme that they name: `segment_ids`: in each row the document numbers never fall; every document has 1 to 1024 positions, and some document has exactly 1024.
All inputs are finite; a program needn't handle non-finite values.
Results may differ from the reference program's by a relative error of at most 0.018.
Values may be sent and summed in bfloat16 or wider, within the bound.
No kernel may reach another device: no remote copies, remote signals or barrier semaphores. Data moves between devices by JAX's collectives and lax.ppermute only.
A program may use at most 384 MiB of HBM per device.

```python
import math
from functools import partial
import jax
import jax.numpy as jnp
import numpy as np
from jax import lax

D = 768
H = 24
P_SIZE = 64
N = 128
KCONV = 4
BLOCK = 256
INNER = 1536
CHANNELS = 1792
PROJ_WIDTH = 3352
LENGTH = 2048
BATCH = 8
DOCS = 3


def steps_of(rng, shape, split, smallest, high):
    def one(position, shards_of):
        draws = jax.random.uniform(jax.random.fold_in(jax.random.fold_in(rng, 6), position), (shards_of,), jnp.float32, smallest / len(split), high / len(split))
        return jnp.repeat(jnp.exp(draws), shape[position] // shards_of).reshape((-1,) + (1,) * (len(shape) - position - 1))

    factor_of = one(*split[0])
    for cut in split[1:]:
        factor_of = factor_of * one(*cut)
    return factor_of


def split_up(count, total, reach, skew):
    weights = [(1 << 20) // math.isqrt(standing ** skew) + 1 for standing in range(2, count + 1)]
    spare, given = total - reach - (count - 1), [1] * (count - 1)
    while spare > 0:
        movable = [i for i in range(count - 1) if given[i] < reach]
        pool, remaining = sum([weights[i] for i in movable]), spare
        for i in movable:
            addition = min(reach - given[i], max(1, remaining * weights[i] // pool), spare)
            given[i] = given[i] + addition
            spare = spare - addition
    return np.array([reach] + given)


def ragged(rng, amount, total, limit, slope):
    if amount == 2:
        one = jax.random.randint(rng, (), max(1, total - limit), min(limit, total - 1) + 1)
        return jnp.stack([one, total - one])
    sizes = jnp.asarray(split_up(amount, total, limit, slope), jnp.int32)
    twos = (amount - 1) // 2
    donor, sink = sizes[1:1 + 2 * twos:2], sizes[2:2 + 2 * twos:2]
    margin = jnp.minimum(donor - 1, limit - sink)
    moved = jax.random.randint(jax.random.fold_in(rng, 1), (twos,), 0, 1 << 20) % (margin + 1)
    sizes = sizes.at[1:1 + 2 * twos:2].set(donor - moved).at[2:2 + 2 * twos:2].set(sink + moved)
    return sizes[jax.random.permutation(jax.random.fold_in(rng, 2), amount)]


def scatter_about(own_key, shape, deviation, reach, split=(), kind=jnp.bfloat16):
    loudness = steps_of(own_key, shape, split, -0.22, 0.18) if split else 1.0
    values = jax.random.normal(own_key, shape, jnp.float32) * deviation * loudness
    return jnp.minimum(jnp.maximum(values, -reach), reach).astype(kind)


def setup_inputs(seed: int = 0) -> dict:
    key_of = jax.random.split(jax.random.key(seed), 13)
    hidden_in = scatter_about(key_of[0], (BATCH, LENGTH, D), 1.0, 6.0, ((0, 4), (1, 8)))
    segment_ids = jax.vmap(lambda own: jnp.searchsorted(jnp.cumsum(ragged(own, DOCS, LENGTH, LENGTH // 2, 0)), jnp.arange(LENGTH), side="right"))(jax.random.split(key_of[1], BATCH)).reshape((BATCH, LENGTH)).astype(jnp.int32)
    cotangent = scatter_about(key_of[2], (BATCH, LENGTH, D), 1.0, 6.0, ((0, 4), (1, 8)))
    norm_gain = jnp.clip(1.0 + 0.1 * jax.random.normal(key_of[3], (D,), jnp.float32), 0.5, 1.5)
    in_proj = scatter_about(key_of[4], (D, PROJ_WIDTH), D ** -0.5, 0.21875)
    conv_weight = scatter_about(key_of[5], (KCONV, CHANNELS), KCONV ** -0.5, 3.0, (), jnp.float32)
    conv_bias = scatter_about(key_of[6], (CHANNELS,), 0.5, 3.0, (), jnp.float32)
    dt_bias = jnp.clip(jax.random.uniform(key_of[7], (H,), jnp.float32, -4.0, 0.0), -4.0, 0.0)
    a_log = jnp.clip(jax.random.uniform(key_of[8], (H,), jnp.float32, -8.0, 1.0), -8.0, 1.0)
    d_skip = jnp.clip(jax.random.uniform(key_of[9], (H,), jnp.float32, 0.5, 1.5), 0.5, 1.5)
    mix_gain = jnp.clip(1.0 + 0.1 * jax.random.normal(key_of[10], (INNER,), jnp.float32), 0.5, 1.5)
    out_proj = scatter_about(key_of[11], (INNER, D), INNER ** -0.5, 0.15625)
    return {"hidden_in": hidden_in, "segment_ids": segment_ids, "cotangent": cotangent, "norm_gain": norm_gain, "in_proj": in_proj, "conv_weight": conv_weight, "conv_bias": conv_bias, "dt_bias": dt_bias, "a_log": a_log, "d_skip": d_skip, "mix_gain": mix_gain, "out_proj": out_proj}


EPSILON = 1e-05
PRECISE = lax.Precision.HIGHEST

@jax.custom_vjp
def low(v):
    return lax.optimization_barrier(v.astype(jnp.bfloat16)).astype(jnp.float32)

@jax.custom_vjp
def low_back(v):
    return v

def low_keep(v):
    return (low(v), None)

def low_pass(kept, grad):
    return (grad,)

def back_keep(v):
    return (v, None)

def back_low(kept, grad):
    return (low(grad),)
low.defvjp(low_keep, low_pass)
low_back.defvjp(back_keep, back_low)

def block_step(a_log, d_skip, carry, inputs):
    state, prev_id = carry
    x_part, b_part, c_part, dt_part, seg_part = inputs
    decay = dt_part * -jnp.exp(a_log)
    cumul = jnp.cumsum(decay, axis=0)
    cum_heads = cumul.T
    positions = jnp.arange(BLOCK)
    inside = (positions[:, None] >= positions[None, :]) & (seg_part[:, None] == seg_part[None, :])
    log_diff = cum_heads[:, :, None] - cum_heads[:, None, :]
    decay_mat = jnp.where(inside[None], jnp.exp(jnp.where(inside[None], log_diff, 0.0)), 0.0)
    scores = low_back(jnp.dot(c_part, b_part.T, precision=PRECISE))
    mixing = low(scores[None] * decay_mat * dt_part.T[:, None, :])
    diag_out = jnp.einsum('htu,uhp->thp', mixing, x_part, precision=PRECISE)
    same_end = seg_part == seg_part[-1]
    end_weight = jnp.where(same_end[:, None], jnp.exp(cumul[-1][None, :] - cumul), 0.0) * dt_part
    weighted = low(x_part * end_weight[:, :, None])
    local_state = low_back(jnp.einsum('uhp,un->hpn', weighted, b_part, precision=PRECISE))
    keep_mask = seg_part == prev_id
    entry_gain = jnp.where(keep_mask[:, None], jnp.exp(cumul), 0.0)
    from_state = low_back(jnp.einsum('tn,hpn->thp', c_part, low(state), precision=PRECISE))
    outputs = diag_out + from_state * entry_gain[:, :, None] + d_skip[None, :, None] * x_part
    end_gain = jnp.where(seg_part[-1] == prev_id, jnp.exp(cumul[-1]), 0.0)
    new_state = end_gain[:, None, None] * state + local_state
    return ((new_state, seg_part[-1]), outputs)

def block_forward(hidden, segment_row, norm_gain, in_proj, conv_weight, conv_bias, dt_bias, a_log, d_skip, mix_gain, out_proj):
    rstd_in = lax.rsqrt(lax.optimization_barrier(jnp.mean(hidden * hidden, axis=-1, keepdims=True)) + EPSILON)
    normed = low(hidden * rstd_in * norm_gain)
    projected = low_back(jnp.dot(normed, in_proj, precision=PRECISE))
    gate_raw = projected[:, :INNER]
    conv_in = low(projected[:, INNER:INNER + CHANNELS])
    dt_raw = projected[:, INNER + CHANNELS:]
    padded = jnp.concatenate([jnp.zeros((KCONV - 1, CHANNELS), jnp.float32), conv_in], axis=0)
    pad_ids = jnp.concatenate([jnp.full((KCONV - 1,), -1, jnp.int32), segment_row], axis=0)
    conv_out = conv_bias + jnp.zeros((LENGTH, CHANNELS), jnp.float32)
    for offset in range(KCONV):
        match = (pad_ids[offset:offset + LENGTH] == segment_row).astype(jnp.float32)
        conv_out = conv_out + conv_weight[offset] * padded[offset:offset + LENGTH] * match[:, None]
    activated = low(jax.nn.silu(conv_out))
    blocks = LENGTH // BLOCK
    x_blocks = activated[:, :INNER].reshape(blocks, BLOCK, H, P_SIZE)
    b_blocks = activated[:, INNER:INNER + N].reshape(blocks, BLOCK, N)
    c_blocks = activated[:, INNER + N:].reshape(blocks, BLOCK, N)
    step_size = jax.nn.softplus(dt_raw + dt_bias)
    dt_blocks = step_size.reshape(blocks, BLOCK, H)
    seg_blocks = segment_row.reshape(blocks, BLOCK)
    stepper = jax.checkpoint(partial(block_step, a_log, d_skip))
    start_carry = (jnp.zeros((H, P_SIZE, N), jnp.float32), jnp.array(-1, jnp.int32))
    _, block_outs = lax.scan(stepper, start_carry, (x_blocks, b_blocks, c_blocks, dt_blocks, seg_blocks))
    ssm_out = low_back(block_outs.reshape(LENGTH, INNER))
    gated_in = ssm_out * jax.nn.silu(gate_raw)
    rstd_mix = lax.rsqrt(lax.optimization_barrier(jnp.mean(gated_in * gated_in, axis=-1, keepdims=True)) + EPSILON)
    normal_out = low(gated_in * rstd_mix * mix_gain)
    return hidden + jnp.dot(normal_out, out_proj, precision=PRECISE)

def reference(hidden_in, segment_ids, cotangent, norm_gain, in_proj, conv_weight, conv_bias, dt_bias, a_log, d_skip, mix_gain, out_proj):
    weights = (norm_gain.astype(jnp.float32), in_proj.astype(jnp.float32), conv_weight.astype(jnp.float32), conv_bias.astype(jnp.float32), dt_bias.astype(jnp.float32), a_log.astype(jnp.float32), d_skip.astype(jnp.float32), mix_gain.astype(jnp.float32), out_proj.astype(jnp.float32))

    def per_sequence(totals, row_inputs):
        hidden_row, segment_row, cot_row = row_inputs

        def forward_fn(hidden, *params):
            return block_forward(hidden, segment_row, *params)
        result, pull_back = jax.vjp(forward_fn, hidden_row.astype(jnp.float32), *weights)
        grads = pull_back(cot_row.astype(jnp.float32))
        new_totals = tuple((total + grad for total, grad in zip(totals, grads[1:])))
        return (new_totals, (result.astype(jnp.bfloat16), grads[0].astype(jnp.bfloat16)))
    start_totals = tuple((jnp.zeros_like(weight) for weight in weights))
    totals, (hidden_out, grad_hidden) = lax.scan(per_sequence, start_totals, (hidden_in, segment_ids, cotangent))
    return (hidden_out, grad_hidden, totals[0], totals[1], totals[2], totals[3], totals[4], totals[5], totals[6], totals[7], totals[8])
```

```python
import jax
import jax.numpy as jnp
from jax import lax
from jax.sharding import PartitionSpec as P

EPSILON = 1e-05


def passed_along(value, axis, steps):
    count = lax.axis_size(axis)
    leading, last = (max(0, -steps), min(count, count - steps))
    return lax.ppermute(value, axis, [(source, source + steps) for source in range(leading, last)])


def exchanged(value, axis, flip):
    count = lax.axis_size(axis)
    return lax.ppermute(value, axis, [(place, place ^ flip) for place in range(count)])


def bit_groups(axis, start, widest):
    count, shift, groups = lax.axis_size(axis), start, []
    while (1 << shift) < count:
        radix = min(widest, count >> shift)
        groups.append((axis, shift, radix))
        shift += radix.bit_length() - 1
    return groups


def all_groups():
    pair = [("seq", 0, 2)]
    return pair + bit_groups("dp", 0, 4) + bit_groups("seq", 1, 4)


def place_in(group):
    axis, shift, radix = group
    return (lax.axis_index(axis) >> shift) & (radix - 1)


def split_sum(value, groups):
    for group in groups:
        axis, shift, radix = group
        place = place_in(group)
        parts = value.reshape((radix, value.shape[0] // radix) + value.shape[1:])
        total = lax.dynamic_index_in_dim(parts, place, 0, False).astype(jnp.float32)
        for k in range(1, radix):
            sent = lax.dynamic_index_in_dim(parts, place ^ k, 0, False).astype(jnp.bfloat16)
            total = total + exchanged(sent, axis, k << shift).astype(jnp.float32)
        value = total
    return value


def spread(value, groups):
    value = value.astype(jnp.bfloat16)
    for group in reversed(groups):
        axis, shift, radix = group
        place = place_in(group)
        whole = jnp.zeros((radix,) + value.shape, value.dtype)
        for k in range(radix):
            piece = value if k == 0 else exchanged(value, axis, k << shift)
            whole = lax.dynamic_update_index_in_dim(whole, piece, place ^ k, 0)
        value = whole.reshape((radix * value.shape[0],) + value.shape[1:])
    return value


def summed_matrix(value):
    groups = all_groups()
    chunks = 1
    for _, _, radix in groups:
        chunks *= radix
    rows, columns = value.shape
    pieces = value.reshape(chunks, rows // chunks, columns)
    return spread(split_sum(pieces, groups), groups).reshape(rows, columns)


def summed_small(parts):
    sizes = [part.size for part in parts]
    flat = jnp.concatenate([part.reshape(-1) for part in parts])
    width = -(-flat.size // 1024) * 1024
    flat = jnp.pad(flat, (0, width - flat.size)).reshape(-1, 128)
    for axis, shift, _ in [("seq", 0, 2)] + bit_groups("dp", 0, 2) + bit_groups("seq", 1, 2):
        flat = flat + exchanged(flat, axis, 1 << shift)
    flat, at, outs = flat.reshape(-1), 0, []
    for part, size in zip(parts, sizes):
        outs.append(flat[at : at + size].reshape(part.shape))
        at += size
    return outs


def halves(value, core):
    half = value.shape[1] // 2
    first, second = value[:, :half], value[:, half:]
    return jnp.where(core == 0, first, second), jnp.where(core == 0, second, first)


def widened(gain):
    return gain[..., None, None]


def pair_gains(end_gain, core):
    other = exchanged(end_gain, "seq", 1)
    gain_first = jnp.where(core == 0, end_gain, other)
    gain_second = jnp.where(core == 0, other, end_gain)
    return gain_first, gain_second


def chip_scan(state, gain, steps, direction):
    chips = lax.axis_size("seq") // 2
    state = passed_along(state.astype(jnp.bfloat16), "seq", 2 * direction).astype(jnp.float32)
    window = 1
    for far in steps:
        later = passed_along(state.astype(jnp.bfloat16), "seq", 2 * window * direction)
        state = state + widened(far) * later.astype(jnp.float32)
        window *= 2
    return state


def chip_gains(gain, direction):
    chips = lax.axis_size("seq") // 2
    gain = passed_along(gain, "seq", 2 * direction)
    steps, window = [], 1
    while window < (chips + 1) // 2:
        steps.append(gain)
        window *= 2
        if window < (chips + 1) // 2:
            gain = gain * passed_along(gain, "seq", window * direction)
    return steps


def scan_states(local, gain_first, gain_second, steps, core, direction):
    near = gain_second if direction > 0 else gain_first
    far = gain_first if direction > 0 else gain_second
    low = local.astype(jnp.bfloat16)
    kept, sent = halves(low, core)
    arrived = exchanged(sent, "seq", 1)
    at_first = jnp.where(core == 0, kept, arrived).astype(jnp.float32)
    at_second = jnp.where(core == 0, arrived, kept).astype(jnp.float32)
    early, late = (at_first, at_second) if direction > 0 else (at_second, at_first)
    near_half, _ = halves(near, core)
    far_half, _ = halves(far, core)
    chip_state = widened(near_half) * early + late
    outer = chip_scan(chip_state, None, [halves(step, core)[0] for step in steps], direction)
    inner = early + widened(far_half) * outer
    is_outer = (core == 0) if direction > 0 else (core == 1)
    mine = jnp.where(is_outer, outer, inner)
    theirs = exchanged(jnp.where(is_outer, inner, outer).astype(jnp.bfloat16), "seq", 1)
    theirs = theirs.astype(jnp.float32)
    return jnp.concatenate(
        [jnp.where(core == 0, mine, theirs), jnp.where(core == 0, theirs, mine)], axis=1
    )


def body(
    hidden_in,
    segment_ids,
    cotangent,
    norm_gain,
    in_proj,
    conv_weight,
    conv_bias,
    dt_bias,
    a_log,
    d_skip,
    mix_gain,
    out_proj,
):
    seq_count, length, model_width = hidden_in.shape
    head_count = dt_bias.shape[0]
    inner_width = mix_gain.shape[0]
    head_size = inner_width // head_count
    channels = conv_bias.shape[0]
    state_size = (channels - inner_width) // 2
    tap_count = conv_weight.shape[0]
    row_count = seq_count * length
    source = hidden_in.astype(jnp.float32)
    rstd_in = lax.rsqrt(jnp.mean(source * source, axis=-1, keepdims=True) + EPSILON)
    unit_in = source * rstd_in
    normed = (unit_in * norm_gain).astype(jnp.bfloat16)
    projected = jnp.dot(
        normed.reshape(row_count, model_width), in_proj, preferred_element_type=jnp.float32
    ).reshape(seq_count, length, -1)
    gate_raw = projected[..., :inner_width]
    conv_in = projected[..., inner_width : inner_width + channels].astype(jnp.bfloat16)
    dt_raw = projected[..., inner_width + channels :]
    seg_float = segment_ids.astype(jnp.float32)
    tail_rows, tail_ids = passed_along(
        (
            conv_in[:, length - (tap_count - 1) :, :],
            seg_float[:, length - (tap_count - 1) :].astype(jnp.bfloat16),
        ),
        "seq",
        1,
    )
    prev_id = tail_ids[:, -1].astype(jnp.float32)
    padded = jnp.concatenate([tail_rows, conv_in], axis=1).astype(jnp.float32)
    pad_ids = jnp.concatenate([tail_ids.astype(jnp.float32), seg_float], axis=1)
    tap_masks = []
    conv_out = conv_bias + jnp.zeros((seq_count, length, channels), jnp.float32)
    for offset in range(tap_count):
        match = (pad_ids[:, offset : offset + length] == seg_float).astype(jnp.float32)[..., None]
        tap_masks.append(match)
        conv_out = conv_out + conv_weight[offset] * padded[:, offset : offset + length] * match
    activated = jax.nn.silu(conv_out).astype(jnp.bfloat16)
    x_vals = activated[..., :inner_width].reshape(seq_count, length, head_count, head_size)
    b_vals = activated[..., inner_width : inner_width + state_size]
    c_vals = activated[..., inner_width + state_size :]
    x_float = x_vals.astype(jnp.float32)
    softplus_in = dt_raw + dt_bias
    step_size = jax.nn.softplus(softplus_in)
    decay_rate = -jnp.exp(a_log)
    cumul = jnp.cumsum(step_size * decay_rate, axis=1)
    cum_heads = jnp.transpose(cumul, (0, 2, 1))
    step_heads = jnp.transpose(step_size, (0, 2, 1))
    positions = jnp.arange(length)
    causal = positions[:, None] >= positions[None, :]
    inside = (causal[None] & (segment_ids[:, :, None] == segment_ids[:, None, :]))[:, None]
    log_diff = cum_heads[..., :, None] - cum_heads[..., None, :]
    decay_mat = jnp.where(inside, jnp.exp(jnp.where(inside, log_diff, 0.0)), 0.0)
    scores = jnp.einsum("stn,sun->stu", c_vals, b_vals, preferred_element_type=jnp.float32)
    mixing = (scores[:, None] * decay_mat * step_heads[:, :, None, :]).astype(jnp.bfloat16)
    diag_out = jnp.einsum("shtu,suhp->sthp", mixing, x_vals, preferred_element_type=jnp.float32)
    last_cum = cumul[:, -1]
    same_end = (seg_float == seg_float[:, -1:])[..., None]
    end_factor = jnp.where(same_end, jnp.exp(last_cum[:, None, :] - cumul), 0.0)
    end_weight = end_factor * step_size
    weighted = (x_float * end_weight[..., None]).astype(jnp.bfloat16)
    local_state = jnp.einsum("suhp,sun->shpn", weighted, b_vals, preferred_element_type=jnp.float32)
    keep_mask = (seg_float == prev_id[:, None])[..., None]
    entry_gain = jnp.where(keep_mask, jnp.exp(cumul), 0.0)
    end_keep = (seg_float[:, -1] == prev_id)[:, None]
    end_gain = jnp.where(end_keep, jnp.exp(last_cum), 0.0)
    core = lax.axis_index("seq") & 1
    gain_first, gain_second = pair_gains(end_gain, core)
    gain_pair = gain_first * gain_second
    steps_on, steps_back = chip_gains(gain_pair, 1), chip_gains(gain_pair, -1)
    state_in = scan_states(local_state, gain_first, gain_second, steps_on, core, 1)
    state_low = state_in.astype(jnp.bfloat16)
    from_state = jnp.einsum("stn,shpn->sthp", c_vals, state_low, preferred_element_type=jnp.float32)
    ssm_heads = diag_out + from_state * entry_gain[..., None] + d_skip[:, None] * x_float
    ssm_out = ssm_heads.reshape(seq_count, length, inner_width)
    gate_act = jax.nn.silu(gate_raw)
    gated_in = ssm_out * gate_act
    rstd_mix = lax.rsqrt(jnp.mean(gated_in * gated_in, axis=-1, keepdims=True) + EPSILON)
    unit_mix = gated_in * rstd_mix
    normal_out = (unit_mix * mix_gain).astype(jnp.bfloat16)
    branch = jnp.dot(
        normal_out.reshape(row_count, inner_width), out_proj, preferred_element_type=jnp.float32
    ).reshape(seq_count, length, model_width)
    hidden_out = (source + branch).astype(jnp.bfloat16)
    upstream = cotangent.astype(jnp.float32)
    flat_cot = cotangent.reshape(row_count, model_width)
    grad_out_turned = jnp.einsum(
        "rd,ri->di",
        flat_cot,
        normal_out.reshape(row_count, inner_width),
        preferred_element_type=jnp.float32,
    ).astype(jnp.bfloat16)
    grad_normal = jnp.dot(flat_cot, out_proj.T, preferred_element_type=jnp.float32).reshape(
        seq_count, length, inner_width
    )
    grad_mix_gain = jnp.sum(grad_normal * unit_mix, axis=(0, 1))
    grad_unit = grad_normal * mix_gain
    grad_gated = rstd_mix * (
        grad_unit - unit_mix * jnp.mean(grad_unit * unit_mix, axis=-1, keepdims=True)
    )
    gate_sig = jax.nn.sigmoid(gate_raw)
    grad_gate = grad_gated * ssm_out * gate_sig * (1.0 + gate_raw * (1.0 - gate_sig))
    grad_gate = grad_gate.astype(jnp.bfloat16).reshape(row_count, inner_width)
    flat_normed = normed.reshape(row_count, model_width)
    grad_in_gate = jnp.einsum(
        "rd,rk->dk", flat_normed, grad_gate, preferred_element_type=jnp.float32
    ).astype(jnp.bfloat16)
    early = summed_matrix(jnp.concatenate([grad_out_turned, grad_in_gate], axis=1))
    grad_y = (
        (grad_gated * gate_act)
        .astype(jnp.bfloat16)
        .reshape(seq_count, length, head_count, head_size)
    )
    grad_yf = grad_y.astype(jnp.float32)
    grad_d_skip = jnp.sum(grad_yf * x_float, axis=(0, 1, 3))
    grad_x = d_skip[:, None] * grad_yf
    grad_raw = (grad_yf * entry_gain[..., None]).astype(jnp.bfloat16)
    grad_entry = jnp.sum(grad_yf * from_state, axis=-1)
    grad_cum = grad_entry * entry_gain
    grad_c = jnp.einsum("sthp,shpn->stn", grad_raw, state_low, preferred_element_type=jnp.float32)
    grad_state_in = jnp.einsum(
        "sthp,stn->shpn", grad_raw, c_vals, preferred_element_type=jnp.float32
    )
    grad_end = scan_states(grad_state_in, gain_first, gain_second, steps_back, core, -1)
    grad_end_gain = jnp.sum(grad_end * state_in, axis=(2, 3))
    grad_last = grad_end_gain * end_gain
    grad_local = grad_end.astype(jnp.bfloat16)
    grad_weighted = jnp.einsum(
        "shpn,sun->suhp", grad_local, b_vals, preferred_element_type=jnp.float32
    )
    grad_b = jnp.einsum("shpn,suhp->sun", grad_local, weighted, preferred_element_type=jnp.float32)
    grad_x = grad_x + grad_weighted * end_weight[..., None]
    grad_weight = jnp.sum(grad_weighted * x_float, axis=-1)
    grad_step = grad_weight * end_factor
    term_end = grad_weight * end_weight
    grad_cum = grad_cum - term_end
    grad_last = grad_last + jnp.sum(term_end, axis=1)
    grad_mixing = jnp.einsum("sthp,suhp->shtu", grad_y, x_vals, preferred_element_type=jnp.float32)
    grad_x = grad_x + jnp.einsum(
        "shtu,sthp->suhp", mixing, grad_y, preferred_element_type=jnp.float32
    )
    shared = grad_mixing * decay_mat
    grad_scores = jnp.sum(shared * step_heads[:, :, None, :], axis=1).astype(jnp.bfloat16)
    grad_c = grad_c + jnp.einsum(
        "stu,sun->stn", grad_scores, b_vals, preferred_element_type=jnp.float32
    )
    grad_b = grad_b + jnp.einsum(
        "stu,stn->sun", grad_scores, c_vals, preferred_element_type=jnp.float32
    )
    flow_term = shared * scores[:, None]
    grad_step_heads = jnp.sum(flow_term, axis=2)
    grad_diff = flow_term * step_heads[:, :, None, :]
    grad_cum_heads = jnp.sum(grad_diff, axis=3) - jnp.sum(grad_diff, axis=2)
    grad_step = grad_step + jnp.transpose(grad_step_heads, (0, 2, 1))
    grad_cum = grad_cum + jnp.transpose(grad_cum_heads, (0, 2, 1))
    last_row = (positions == length - 1).astype(jnp.float32)
    grad_cum = grad_cum + last_row[None, :, None] * grad_last[:, None, :]
    grad_decay = jnp.flip(jnp.cumsum(jnp.flip(grad_cum, 1), axis=1), 1)
    grad_step = grad_step + grad_decay * decay_rate
    grad_a_log = jnp.sum(grad_decay * step_size, axis=(0, 1)) * decay_rate
    grad_soft = grad_step * jax.nn.sigmoid(softplus_in)
    grad_dt_bias = jnp.sum(grad_soft, axis=(0, 1))
    grad_act = jnp.concatenate(
        [grad_x.reshape(seq_count, length, inner_width), grad_b, grad_c], axis=-1
    )
    conv_sig = jax.nn.sigmoid(conv_out)
    grad_conv = grad_act * conv_sig * (1.0 + conv_out * (1.0 - conv_sig))
    grad_conv_bias = jnp.sum(grad_conv, axis=(0, 1))
    tap_grads = []
    grad_padded = jnp.zeros((seq_count, length + tap_count - 1, channels), jnp.float32)
    for offset in range(tap_count):
        masked = grad_conv * tap_masks[offset]
        tap_grads.append(jnp.sum(masked * padded[:, offset : offset + length], axis=(0, 1)))
        grad_padded = grad_padded + jnp.pad(
            conv_weight[offset] * masked, ((0, 0), (offset, tap_count - 1 - offset), (0, 0))
        )
    grad_conv_weight = jnp.stack(tap_grads, axis=0)
    back_rows = passed_along(
        grad_padded[:, : tap_count - 1].astype(jnp.bfloat16), "seq", -1
    ).astype(jnp.float32)
    grad_conv_in = grad_padded[:, tap_count - 1 :] + jnp.pad(
        back_rows, ((0, 0), (length - (tap_count - 1), 0), (0, 0))
    )
    spare = -head_count % 128
    grad_late = (
        jnp.concatenate(
            [grad_conv_in, jnp.pad(grad_soft, ((0, 0), (0, 0), (0, spare)))], axis=-1
        )
        .astype(jnp.bfloat16)
        .reshape(row_count, -1)
    )
    grad_in_late = jnp.einsum(
        "rd,rk->dk", flat_normed, grad_late, preferred_element_type=jnp.float32
    ).astype(jnp.bfloat16)
    late = summed_matrix(grad_in_late)
    grad_projected = jnp.concatenate([grad_gate, grad_late[:, : channels + head_count]], axis=1)
    grad_normed = jnp.dot(grad_projected, in_proj.T, preferred_element_type=jnp.float32).reshape(
        seq_count, length, model_width
    )
    grad_norm_gain = jnp.sum(grad_normed * unit_in, axis=(0, 1))
    grad_unit_in = grad_normed * norm_gain
    grad_source = rstd_in * (
        grad_unit_in - unit_in * jnp.mean(grad_unit_in * unit_in, axis=-1, keepdims=True)
    )
    grad_hidden = (upstream + grad_source).astype(jnp.bfloat16)
    (
        total_norm,
        total_taps,
        total_bias,
        total_dt,
        total_alog,
        total_skip,
        total_mix,
    ) = summed_small(
        (
            grad_norm_gain,
            grad_conv_weight,
            grad_conv_bias,
            grad_dt_bias,
            grad_a_log,
            grad_d_skip,
            grad_mix_gain,
        )
    )
    total_out = early[:, :inner_width].T.astype(jnp.float32)
    total_in = jnp.concatenate(
        [early[:, inner_width:], late[:, : channels + head_count]], axis=1
    ).astype(jnp.float32)
    return (
        hidden_out,
        grad_hidden,
        total_norm,
        total_in,
        total_taps,
        total_bias,
        total_dt,
        total_alog,
        total_skip,
        total_mix,
        total_out,
    )


def solution(mesh):
    return jax.shard_map(
        body,
        mesh=mesh,
        in_specs=(
            P("dp", "seq", None),
            P("dp", "seq"),
            P("dp", "seq", None),
            P(),
            P(),
            P(),
            P(),
            P(),
            P(),
            P(),
            P(),
            P(),
        ),
        out_specs=(
            P("dp", "seq", None),
            P("dp", "seq", None),
            P(),
            P(),
            P(),
            P(),
            P(),
            P(),
            P(),
            P(),
            P(),
        ),
        check_vma=False,
    )
```

```python
import jax
import jax.numpy as jnp
from jax import lax
from jax.sharding import PartitionSpec as P

EPSILON = 1e-05


def passed_along(value, axis, steps):
    count = lax.axis_size(axis)
    leading, last = (max(0, -steps), min(count, count - steps))
    return lax.ppermute(value, axis, [(source, source + steps) for source in range(leading, last)])


def exchanged(value, axis, flip):
    count = lax.axis_size(axis)
    return lax.ppermute(value, axis, [(place, place ^ flip) for place in range(count)])


def bit_groups(axis, start, widest):
    count, shift, groups = lax.axis_size(axis), start, []
    while (1 << shift) < count:
        radix = min(widest, count >> shift)
        groups.append((axis, shift, radix))
        shift += radix.bit_length() - 1
    return groups


def all_groups():
    pair = [("seq", 0, 2)]
    return pair + bit_groups("dp", 0, 4) + bit_groups("seq", 1, 4)


def place_in(group):
    axis, shift, radix = group
    return (lax.axis_index(axis) >> shift) & (radix - 1)


def split_sum(value, groups):
    for group in groups:
        axis, shift, radix = group
        place = place_in(group)
        parts = value.reshape((radix, value.shape[0] // radix) + value.shape[1:])
        total = lax.dynamic_index_in_dim(parts, place, 0, False).astype(jnp.float32)
        for k in range(1, radix):
            sent = lax.dynamic_index_in_dim(parts, place ^ k, 0, False).astype(jnp.bfloat16)
            total = total + exchanged(sent, axis, k << shift).astype(jnp.float32)
        value = total
    return value


def in_order(pieces, place):
    bit = 1
    while bit < len(pieces):
        swap = (place & bit) != 0
        pieces = [jnp.where(swap, pieces[j ^ bit], pieces[j]) for j in range(len(pieces))]
        bit *= 2
    return jnp.concatenate(pieces, axis=0)


def spread(value, groups):
    value = value.astype(jnp.bfloat16)
    for group in reversed(groups):
        axis, shift, radix = group
        pieces = [value] + [exchanged(value, axis, k << shift) for k in range(1, radix)]
        value = in_order(pieces, place_in(group))
    return value


def in_chunks(value, groups):
    chunks = 1
    for _, _, radix in groups:
        chunks *= radix
    rows, columns = value.shape
    return value.reshape(chunks, rows // chunks, columns)


def after(value, *others):
    return lax.optimization_barrier((value,) + others)


def summed_small(parts):
    sizes = [part.size for part in parts]
    flat = jnp.concatenate([part.reshape(-1) for part in parts])
    width = -(-flat.size // 1024) * 1024
    flat = jnp.pad(flat, (0, width - flat.size)).reshape(-1, 128)
    for axis, shift, _ in [("seq", 0, 2)] + bit_groups("dp", 0, 2) + bit_groups("seq", 1, 2):
        flat = flat + exchanged(flat, axis, 1 << shift)
    flat, at, outs = flat.reshape(-1), 0, []
    for part, size in zip(parts, sizes):
        outs.append(flat[at : at + size].reshape(part.shape))
        at += size
    return outs


def halves(value, core):
    half = value.shape[1] // 2
    first, second = value[:, :half], value[:, half:]
    return jnp.where(core == 0, first, second), jnp.where(core == 0, second, first)


def widened(gain):
    return gain[..., None, None]


def pair_gains(end_gain, core):
    other = exchanged(end_gain, "seq", 1)
    gain_first = jnp.where(core == 0, end_gain, other)
    gain_second = jnp.where(core == 0, other, end_gain)
    return gain_first, gain_second


def chip_scan(state, steps, direction, beside):
    state = passed_along(state.astype(jnp.bfloat16), "seq", 2 * direction)
    state, beside = after(state, beside)
    state = state.astype(jnp.float32)
    window = 1
    for far in steps:
        later = passed_along(state.astype(jnp.bfloat16), "seq", 2 * window * direction)
        state = state + widened(far) * later.astype(jnp.float32)
        window *= 2
    return state, beside


def chip_gains(gain, direction):
    chips = lax.axis_size("seq") // 2
    gain = passed_along(gain, "seq", 2 * direction)
    steps, window = [], 1
    while window < (chips + 1) // 2:
        steps.append(gain)
        window *= 2
        if window < (chips + 1) // 2:
            gain = gain * passed_along(gain, "seq", window * direction)
    return steps


def scan_states(local, gain_first, gain_second, steps, core, direction, beside):
    near = gain_second if direction > 0 else gain_first
    far = gain_first if direction > 0 else gain_second
    low = local.astype(jnp.bfloat16)
    kept, sent = halves(low, core)
    arrived = exchanged(sent, "seq", 1)
    at_first = jnp.where(core == 0, kept, arrived).astype(jnp.float32)
    at_second = jnp.where(core == 0, arrived, kept).astype(jnp.float32)
    early, late = (at_first, at_second) if direction > 0 else (at_second, at_first)
    near_half, _ = halves(near, core)
    far_half, _ = halves(far, core)
    chip_state = widened(near_half) * early + late
    steps = [halves(step, core)[0] for step in steps]
    outer, beside = chip_scan(chip_state, steps, direction, beside)
    inner = early + widened(far_half) * outer
    is_outer = (core == 0) if direction > 0 else (core == 1)
    mine = jnp.where(is_outer, outer, inner)
    theirs = exchanged(jnp.where(is_outer, inner, outer).astype(jnp.bfloat16), "seq", 1)
    theirs = theirs.astype(jnp.float32)
    whole = jnp.concatenate(
        [jnp.where(core == 0, mine, theirs), jnp.where(core == 0, theirs, mine)], axis=1
    )
    return whole, beside


def body(
    hidden_in,
    segment_ids,
    cotangent,
    norm_gain,
    in_proj,
    conv_weight,
    conv_bias,
    dt_bias,
    a_log,
    d_skip,
    mix_gain,
    out_proj,
):
    seq_count, length, model_width = hidden_in.shape
    head_count = dt_bias.shape[0]
    inner_width = mix_gain.shape[0]
    head_size = inner_width // head_count
    channels = conv_bias.shape[0]
    state_size = (channels - inner_width) // 2
    tap_count = conv_weight.shape[0]
    row_count = seq_count * length
    source = hidden_in.astype(jnp.float32)
    rstd_in = lax.rsqrt(jnp.mean(source * source, axis=-1, keepdims=True) + EPSILON)
    unit_in = source * rstd_in
    normed = (unit_in * norm_gain).astype(jnp.bfloat16)
    projected = jnp.dot(
        normed.reshape(row_count, model_width), in_proj, preferred_element_type=jnp.float32
    ).reshape(seq_count, length, -1)
    gate_raw = projected[..., :inner_width]
    conv_in = projected[..., inner_width : inner_width + channels].astype(jnp.bfloat16)
    dt_raw = projected[..., inner_width + channels :]
    seg_float = segment_ids.astype(jnp.float32)
    tail_rows, tail_ids = passed_along(
        (
            conv_in[:, length - (tap_count - 1) :, :],
            seg_float[:, length - (tap_count - 1) :].astype(jnp.bfloat16),
        ),
        "seq",
        1,
    )
    prev_id = tail_ids[:, -1].astype(jnp.float32)
    padded = jnp.concatenate([tail_rows, conv_in], axis=1).astype(jnp.float32)
    pad_ids = jnp.concatenate([tail_ids.astype(jnp.float32), seg_float], axis=1)
    tap_masks = []
    conv_out = conv_bias + jnp.zeros((seq_count, length, channels), jnp.float32)
    for offset in range(tap_count):
        match = (pad_ids[:, offset : offset + length] == seg_float).astype(jnp.float32)[..., None]
        tap_masks.append(match)
        conv_out = conv_out + conv_weight[offset] * padded[:, offset : offset + length] * match
    activated = jax.nn.silu(conv_out).astype(jnp.bfloat16)
    x_vals = activated[..., :inner_width].reshape(seq_count, length, head_count, head_size)
    b_vals = activated[..., inner_width : inner_width + state_size]
    c_vals = activated[..., inner_width + state_size :]
    x_float = x_vals.astype(jnp.float32)
    softplus_in = dt_raw + dt_bias
    step_size = jax.nn.softplus(softplus_in)
    decay_rate = -jnp.exp(a_log)
    cumul = jnp.cumsum(step_size * decay_rate, axis=1)
    cum_heads = jnp.transpose(cumul, (0, 2, 1))
    step_heads = jnp.transpose(step_size, (0, 2, 1))
    positions = jnp.arange(length)
    causal = positions[:, None] >= positions[None, :]
    inside = (causal[None] & (segment_ids[:, :, None] == segment_ids[:, None, :]))[:, None]
    log_diff = cum_heads[..., :, None] - cum_heads[..., None, :]
    decay_mat = jnp.where(inside, jnp.exp(jnp.where(inside, log_diff, 0.0)), 0.0)
    scores = jnp.einsum("stn,sun->stu", c_vals, b_vals, preferred_element_type=jnp.float32)
    mixing = (scores[:, None] * decay_mat * step_heads[:, :, None, :]).astype(jnp.bfloat16)
    diag_out = jnp.einsum("shtu,suhp->sthp", mixing, x_vals, preferred_element_type=jnp.float32)
    last_cum = cumul[:, -1]
    same_end = (seg_float == seg_float[:, -1:])[..., None]
    end_factor = jnp.where(same_end, jnp.exp(last_cum[:, None, :] - cumul), 0.0)
    end_weight = end_factor * step_size
    weighted = (x_float * end_weight[..., None]).astype(jnp.bfloat16)
    local_state = jnp.einsum("suhp,sun->shpn", weighted, b_vals, preferred_element_type=jnp.float32)
    keep_mask = (seg_float == prev_id[:, None])[..., None]
    entry_gain = jnp.where(keep_mask, jnp.exp(cumul), 0.0)
    end_keep = (seg_float[:, -1] == prev_id)[:, None]
    end_gain = jnp.where(end_keep, jnp.exp(last_cum), 0.0)
    core = lax.axis_index("seq") & 1
    gain_first, gain_second = pair_gains(end_gain, core)
    gain_pair = gain_first * gain_second
    steps_on, steps_back = chip_gains(gain_pair, 1), chip_gains(gain_pair, -1)
    state_in, diag_out = scan_states(
        local_state, gain_first, gain_second, steps_on, core, 1, diag_out
    )
    state_low = state_in.astype(jnp.bfloat16)
    from_state = jnp.einsum("stn,shpn->sthp", c_vals, state_low, preferred_element_type=jnp.float32)
    ssm_heads = diag_out + from_state * entry_gain[..., None] + d_skip[:, None] * x_float
    ssm_out = ssm_heads.reshape(seq_count, length, inner_width)
    gate_act = jax.nn.silu(gate_raw)
    gated_in = ssm_out * gate_act
    rstd_mix = lax.rsqrt(jnp.mean(gated_in * gated_in, axis=-1, keepdims=True) + EPSILON)
    unit_mix = gated_in * rstd_mix
    normal_out = (unit_mix * mix_gain).astype(jnp.bfloat16)
    branch = jnp.dot(
        normal_out.reshape(row_count, inner_width), out_proj, preferred_element_type=jnp.float32
    ).reshape(seq_count, length, model_width)
    hidden_out = (source + branch).astype(jnp.bfloat16)
    upstream = cotangent.astype(jnp.float32)
    flat_cot = cotangent.reshape(row_count, model_width)
    grad_out_part = jnp.einsum(
        "ri,rd->id",
        normal_out.reshape(row_count, inner_width),
        flat_cot,
        preferred_element_type=jnp.float32,
    ).astype(jnp.bfloat16)
    grad_normal = jnp.dot(flat_cot, out_proj.T, preferred_element_type=jnp.float32).reshape(
        seq_count, length, inner_width
    )
    grad_mix_gain = jnp.sum(grad_normal * unit_mix, axis=(0, 1))
    grad_unit = grad_normal * mix_gain
    grad_gated = rstd_mix * (
        grad_unit - unit_mix * jnp.mean(grad_unit * unit_mix, axis=-1, keepdims=True)
    )
    gate_sig = jax.nn.sigmoid(gate_raw)
    grad_gate = grad_gated * ssm_out * gate_sig * (1.0 + gate_raw * (1.0 - gate_sig))
    grad_gate = grad_gate.astype(jnp.bfloat16).reshape(row_count, inner_width)
    flat_normed = normed.reshape(row_count, model_width)
    grad_in_gate = jnp.einsum(
        "rk,rd->kd", grad_gate, flat_normed, preferred_element_type=jnp.float32
    ).astype(jnp.bfloat16)
    groups = all_groups()
    early = in_chunks(jnp.concatenate([grad_in_gate, grad_out_part], axis=0), groups)
    early = split_sum(early, groups[:1])
    grad_y = (
        (grad_gated * gate_act)
        .astype(jnp.bfloat16)
        .reshape(seq_count, length, head_count, head_size)
    )
    grad_yf = grad_y.astype(jnp.float32)
    grad_d_skip = jnp.sum(grad_yf * x_float, axis=(0, 1, 3))
    grad_x = d_skip[:, None] * grad_yf
    grad_raw = (grad_yf * entry_gain[..., None]).astype(jnp.bfloat16)
    grad_entry = jnp.sum(grad_yf * from_state, axis=-1)
    grad_cum = grad_entry * entry_gain
    grad_c = jnp.einsum("sthp,shpn->stn", grad_raw, state_low, preferred_element_type=jnp.float32)
    grad_state_in = jnp.einsum(
        "sthp,stn->shpn", grad_raw, c_vals, preferred_element_type=jnp.float32
    )
    grad_mixing = jnp.einsum("sthp,suhp->shtu", grad_y, x_vals, preferred_element_type=jnp.float32)
    grad_diag = jnp.einsum("shtu,sthp->suhp", mixing, grad_y, preferred_element_type=jnp.float32)
    grad_state_in, early = after(grad_state_in, early)
    early = split_sum(early, groups[1:2])
    grad_end, grad_diag = scan_states(
        grad_state_in, gain_first, gain_second, steps_back, core, -1, grad_diag
    )
    grad_end, early = after(grad_end, early)
    early = split_sum(early, groups[2:])
    grad_end_gain = jnp.sum(grad_end * state_in, axis=(2, 3))
    grad_last = grad_end_gain * end_gain
    grad_local = grad_end.astype(jnp.bfloat16)
    grad_weighted = jnp.einsum(
        "shpn,sun->suhp", grad_local, b_vals, preferred_element_type=jnp.float32
    )
    grad_b = jnp.einsum("shpn,suhp->sun", grad_local, weighted, preferred_element_type=jnp.float32)
    grad_x = grad_x + grad_weighted * end_weight[..., None]
    grad_weight = jnp.sum(grad_weighted * x_float, axis=-1)
    grad_step = grad_weight * end_factor
    term_end = grad_weight * end_weight
    grad_cum = grad_cum - term_end
    grad_last = grad_last + jnp.sum(term_end, axis=1)
    grad_x = grad_x + grad_diag
    shared = grad_mixing * decay_mat
    grad_scores = jnp.sum(shared * step_heads[:, :, None, :], axis=1).astype(jnp.bfloat16)
    grad_c = grad_c + jnp.einsum(
        "stu,sun->stn", grad_scores, b_vals, preferred_element_type=jnp.float32
    )
    grad_b = grad_b + jnp.einsum(
        "stu,stn->sun", grad_scores, c_vals, preferred_element_type=jnp.float32
    )
    flow_term = shared * scores[:, None]
    grad_step_heads = jnp.sum(flow_term, axis=2)
    grad_diff = flow_term * step_heads[:, :, None, :]
    grad_cum_heads = jnp.sum(grad_diff, axis=3) - jnp.sum(grad_diff, axis=2)
    grad_step = grad_step + jnp.transpose(grad_step_heads, (0, 2, 1))
    grad_cum = grad_cum + jnp.transpose(grad_cum_heads, (0, 2, 1))
    last_row = (positions == length - 1).astype(jnp.float32)
    grad_cum = grad_cum + last_row[None, :, None] * grad_last[:, None, :]
    grad_decay = jnp.flip(jnp.cumsum(jnp.flip(grad_cum, 1), axis=1), 1)
    grad_step = grad_step + grad_decay * decay_rate
    grad_a_log = jnp.sum(grad_decay * step_size, axis=(0, 1)) * decay_rate
    grad_soft = grad_step * jax.nn.sigmoid(softplus_in)
    grad_dt_bias = jnp.sum(grad_soft, axis=(0, 1))
    grad_act = jnp.concatenate(
        [grad_x.reshape(seq_count, length, inner_width), grad_b, grad_c], axis=-1
    )
    grad_act, early = after(grad_act, early)
    early = spread(early, groups[2:])
    conv_sig = jax.nn.sigmoid(conv_out)
    grad_conv = grad_act * conv_sig * (1.0 + conv_out * (1.0 - conv_sig))
    grad_conv_bias = jnp.sum(grad_conv, axis=(0, 1))
    tap_grads = []
    grad_padded = jnp.zeros((seq_count, length + tap_count - 1, channels), jnp.float32)
    for offset in range(tap_count):
        masked = grad_conv * tap_masks[offset]
        tap_grads.append(jnp.sum(masked * padded[:, offset : offset + length], axis=(0, 1)))
        grad_padded = grad_padded + jnp.pad(
            conv_weight[offset] * masked, ((0, 0), (offset, tap_count - 1 - offset), (0, 0))
        )
    grad_conv_weight = jnp.stack(tap_grads, axis=0)
    back_rows = passed_along(
        grad_padded[:, : tap_count - 1].astype(jnp.bfloat16), "seq", -1
    ).astype(jnp.float32)
    grad_conv_in = grad_padded[:, tap_count - 1 :] + jnp.pad(
        back_rows, ((0, 0), (length - (tap_count - 1), 0), (0, 0))
    )
    grad_conv_in, early = after(grad_conv_in.astype(jnp.bfloat16), early)
    early = spread(early, groups[1:2])
    flat_conv = grad_conv_in.reshape(row_count, channels)
    flat_soft = grad_soft.astype(jnp.bfloat16).reshape(row_count, head_count)
    late = jnp.einsum(
        "rk,rd->kd", flat_conv, flat_normed, preferred_element_type=jnp.float32
    ).astype(jnp.bfloat16)
    grad_in_soft = jnp.einsum(
        "rk,rd->kd", flat_soft, flat_normed, preferred_element_type=jnp.float32
    )
    late, early = after(late, early)
    late = spread(split_sum(in_chunks(late, groups), groups), groups)
    late = late.reshape(channels, model_width)
    early = spread(early, groups[:1]).reshape(2 * inner_width, model_width)
    grad_projected = jnp.concatenate([grad_gate, flat_conv, flat_soft], axis=1)
    grad_normed = jnp.dot(grad_projected, in_proj.T, preferred_element_type=jnp.float32).reshape(
        seq_count, length, model_width
    )
    grad_norm_gain = jnp.sum(grad_normed * unit_in, axis=(0, 1))
    grad_unit_in = grad_normed * norm_gain
    grad_source = rstd_in * (
        grad_unit_in - unit_in * jnp.mean(grad_unit_in * unit_in, axis=-1, keepdims=True)
    )
    grad_hidden = (upstream + grad_source).astype(jnp.bfloat16)
    (
        total_norm,
        total_taps,
        total_bias,
        total_dt,
        total_alog,
        total_skip,
        total_mix,
        total_soft,
    ) = summed_small(
        (
            grad_norm_gain,
            grad_conv_weight,
            grad_conv_bias,
            grad_dt_bias,
            grad_a_log,
            grad_d_skip,
            grad_mix_gain,
            grad_in_soft,
        )
    )
    total_out = early[inner_width:].astype(jnp.float32)
    total_in = jnp.concatenate(
        [
            early[:inner_width].astype(jnp.float32),
            late.astype(jnp.float32),
            total_soft,
        ],
        axis=0,
    ).T
    return (
        hidden_out,
        grad_hidden,
        total_norm,
        total_in,
        total_taps,
        total_bias,
        total_dt,
        total_alog,
        total_skip,
        total_mix,
        total_out,
    )


def solution(mesh):
    return jax.shard_map(
        body,
        mesh=mesh,
        in_specs=(
            P("dp", "seq", None),
            P("dp", "seq"),
            P("dp", "seq", None),
            P(),
            P(),
            P(),
            P(),
            P(),
            P(),
            P(),
            P(),
            P(),
        ),
        out_specs=(
            P("dp", "seq", None),
            P("dp", "seq", None),
            P(),
            P(),
            P(),
            P(),
            P(),
            P(),
            P(),
            P(),
            P(),
        ),
        check_vma=False,
    )
```
